32 devices in a mesh: clip: 2 (over y), height: 4 (over z), head: 4 (over x, core).
Axes of the slice: x: 2, y: 2, z: 4, core: 2. Of those that a mesh axis runs over, the one named last changes fastest.
Arguments:
- tokens: bfloat16 [8, 192, 5120], P(('clip', 'height'), None, 'head'), parts along dimension 0, may hold values from -6 to 6
- in_sign: int32 [5120], replicated, may hold values from 0 to 1
- qkv_codes: int32 [640, 3, 3072], P(None, None, 'head'), may hold values from 0 to 65535
- qkv_scale: float32 [3, 3072], P(None, 'head'), may hold values from 0.3 to 3
- qkv_sign: int32 [3, 3072], P(None, 'head'), may hold values from 0 to 1
- windows: int32 [8, 3, 27], P(('clip', 'height')), parts along dimension 0, may hold values from 0 to 11, as said below
- oin_sign: int32 [3072], P('head'), may hold values from 0 to 1
- out_codes: int32 [384, 5120], P('head'), may hold values from 0 to 65535
- out_scale: float32 [5120], replicated, may hold values from 2 to 20
- out_sign: int32 [5120], replicated, may hold values from 0 to 1
Outputs:
- attention_out: bfloat16 [8, 192, 5120], P(('clip', 'height'), 'head'), parts along dimension 0
The draws below stay inside these ranges and needn't reach their ends.
There are 2 independent parts, one for each index of `clip`. The reference program is written for one: setup_inputs(seed, part) draws one part's arguments, and reference() takes and returns one part's arrays. A program takes and returns all parts, laid end to end along the dimension named above; an argument that names none is the same for every part. Nothing has to cross between parts.
Inputs may be any that keep to these rules, and one draw needn't show every extreme that they name: `windows`: each row lists the query tile itself and 26 further entries, each one of the 27 tiles of the 3 x 3 x 3 block of tiles centred on the query tile (each of the three coordinates clipped into the grid of 1 x 4 x 3 tiles); entries may repeat and appear in any order.
All inputs are finite; a program needn't handle non-finite values.
Results may differ from the reference program's by a relative error of at most 0.015.
Values may be sent and summed in bfloat16 or wider, within the bound.
A program may use at most 128 MiB of HBM per device.

```python
import math
import jax
import jax.numpy as jnp
import numpy as np
from jax import lax

D = 5120
HD = 128
HEADS = 24
HAD = 128
HROWS = 4
WTILES = 3
TTILES = 1
SLABS = 4
TILE = 64
QTILES = 3
TOK_DEV = 192
TOKENS = 768
N_HEAD = 4


def draw_windows(key, part):
    slab_index = jnp.arange(SLABS, dtype=jnp.int32)[:, None, None, None, None]
    col_index = jnp.arange(WTILES, dtype=jnp.int32)[None, :, None, None, None]
    stepping = jnp.arange(3, dtype=jnp.int32) - 1
    time_all = jnp.clip(slab_index // HROWS + stepping[None, None, :, None, None], 0, TTILES - 1)
    row_all = jnp.clip(slab_index % HROWS + stepping[None, None, None, :, None], 0, HROWS - 1)
    col_all = jnp.clip(col_index + stepping[None, None, None, None, :], 0, WTILES - 1)
    tile_ids = ((time_all * HROWS + row_all) * WTILES + col_all).reshape(SLABS * WTILES, 27)
    pick_key = jax.random.fold_in(key, 11)
    order_key = jax.random.fold_in(key, 23)
    picks = jax.random.randint(pick_key, (SLABS * WTILES, 27), 0, 27).astype(jnp.int32)
    picks = picks.at[:, 0].set(13)
    chosen = jnp.take_along_axis(tile_ids, picks, axis=1)
    row_keys = jax.random.split(order_key, SLABS * WTILES)
    orders = jax.vmap(lambda one_key: jax.random.permutation(one_key, 27))(row_keys)
    shuffled = jnp.take_along_axis(chosen, orders.astype(jnp.int32), axis=1)
    return shuffled.reshape(SLABS, WTILES, 27).astype(jnp.int32)


def with_ends(entries, own_key, low, high):
    spot = [jax.random.randint(jax.random.fold_in(own_key, axis), (), 0, length) for axis, length in enumerate(entries.shape)]
    widest = entries.shape.index(max(entries.shape))
    next_to = spot[:widest] + [(spot[widest] + 1) % entries.shape[widest]] + spot[widest + 1:]
    return entries.at[tuple(spot)].set(low).at[tuple(next_to)].set(high)


def block_scale(stream_key, shape, shards, smallest, top_value):
    def one(position, blocks):
        heights = jax.random.uniform(jax.random.fold_in(jax.random.fold_in(stream_key, 6), position), (blocks,), jnp.float32, smallest / len(shards), top_value / len(shards))
        return jnp.repeat(jnp.exp(heights), shape[position] // blocks).reshape((-1,) + (1,) * (len(shape) - position - 1))

    level = one(*shards[0])
    for cut in shards[1:]:
        level = level * one(*cut)
    return level


def centred(stream_key, shape, deviation, limit, cuts=(), held_as=jnp.bfloat16):
    values = jax.random.normal(stream_key, shape, jnp.float32) * deviation
    if len(cuts) > 0:
        values = block_scale(stream_key, shape, cuts, -0.22, 0.18) * values
    return jnp.clip(values, min=-limit, max=limit).astype(held_as)


def setup_inputs(seed: int = 0, part: int = 0) -> dict:
    splits = jax.random.split(jax.random.key(seed), 11)
    own_keys = jax.random.split(jax.random.fold_in(splits[10], part), 11)
    return {
        "tokens": centred(own_keys[0], (SLABS, TOK_DEV, D), 1.0, 6.0, ((0, 4), (2, 4))),
        "in_sign": with_ends(jax.random.randint(splits[1], (D,), 0, 2), jax.random.fold_in(splits[1], 1), 0, 1).astype(jnp.int32),
        "qkv_codes": with_ends(jax.random.randint(splits[2], (D // 8, 3, HEADS * HD), 0, 65536), jax.random.fold_in(splits[2], 1), 0, 65535).astype(jnp.int32),
        "qkv_scale": jnp.clip(jnp.exp(math.log(3.0) - 2.3025851 * jax.random.uniform(splits[3], (3, HEADS * HD), jnp.float32) ** block_scale(splits[3], (3, HEADS * HD), ((1, 4),), -0.2, 0.2)), 0.3, 3.0),
        "qkv_sign": with_ends(jax.random.randint(splits[4], (3, HEADS * HD), 0, 2), jax.random.fold_in(splits[4], 1), 0, 1).astype(jnp.int32),
        "windows": draw_windows(jax.random.fold_in(jax.random.fold_in(splits[10], part), 71), part),
        "oin_sign": with_ends(jax.random.randint(splits[6], (HEADS * HD,), 0, 2), jax.random.fold_in(splits[6], 1), 0, 1).astype(jnp.int32),
        "out_codes": with_ends(jax.random.randint(splits[7], (HEADS * HD // 8, D), 0, 65536), jax.random.fold_in(splits[7], 1), 0, 65535).astype(jnp.int32),
        "out_scale": jnp.clip(jnp.exp(jax.random.uniform(splits[8], (D,), jnp.float32, math.log(2.0), math.log(20.0))), 2.0, 20.0),
        "out_sign": with_ends(jax.random.randint(splits[9], (D,), 0, 2), jax.random.fold_in(splits[9], 1), 0, 1).astype(jnp.int32),
    }


epsilon = 1e-06

def sylvester(order_size):
    matrix_now = np.ones((1, 1), np.float32)
    seed_pair = np.array([[1.0, 1.0], [1.0, -1.0]], np.float32)
    while matrix_now.shape[0] < order_size:
        matrix_now = np.kron(matrix_now, seed_pair)
    return matrix_now

def signed(sign_bits):
    return (2 * sign_bits - 1).astype(jnp.float32)

def unpack(packed):
    powers = np.array([4 ** k for k in range(8)], np.int32)
    powers = jnp.asarray(powers.reshape((1, 8) + (1,) * (packed.ndim - 1)), jnp.int32)
    digits = packed[:, None] // powers % 4
    return digits.reshape((packed.shape[0] * 8,) + packed.shape[1:])

def levels(packed, column_scale, fan_in):
    return ((unpack(packed).astype(jnp.float32) - 1.5) * (column_scale * fan_in ** (-0.5))).astype(jnp.bfloat16)

def rotate_exact(matrix_in):
    row_count, columns = matrix_in.shape
    hadamard = jnp.asarray(sylvester(HAD), jnp.float32)
    grouped = matrix_in.astype(jnp.float32).reshape(row_count, columns // HAD, HAD)
    turned = jnp.einsum('rbi,ij->rbj', grouped, hadamard, precision=lax.Precision.HIGHEST)
    return turned.reshape(row_count, columns) * HAD ** (-0.5)

def normalize(vectors):
    return vectors / jnp.sqrt(lax.optimization_barrier(jnp.mean(vectors * vectors, axis=-1, keepdims=True)) + epsilon)

def reference(tokens, in_sign, qkv_codes, qkv_scale, qkv_sign, windows, oin_sign, out_codes, out_scale, out_sign):
    flat_tokens = tokens.reshape(TOKENS, D)
    turned = rotate_exact(flat_tokens.astype(jnp.float32) * signed(in_sign)).astype(jnp.bfloat16)
    qkv_weight = levels(qkv_codes, qkv_scale, D).reshape(D, 3 * HEADS * HD)
    projected = jnp.dot(turned, qkv_weight, preferred_element_type=jnp.float32)
    mixed = rotate_exact(projected) * signed(qkv_sign).reshape(-1)
    mixed = mixed.reshape(TOKENS, 3, HEADS, HD)
    queries = normalize(mixed[:, 0]).astype(jnp.bfloat16).reshape(SLABS, TOK_DEV, HEADS, HD)
    key_rows = normalize(mixed[:, 1]).astype(jnp.bfloat16).reshape(SLABS, TOK_DEV, HEADS, HD)
    value_rows = mixed[:, 2].astype(jnp.bfloat16).reshape(SLABS, TOK_DEV, HEADS, HD)
    padding = jnp.zeros((5, TOK_DEV, HEADS, HD), jnp.bfloat16)
    keys_padded = jnp.concatenate([padding, key_rows, padding], 0)
    values_padded = jnp.concatenate([padding, value_rows, padding], 0)
    local_tiles = jnp.arange(11 * QTILES, dtype=jnp.int32)

    def attend(tile_row):
        near_keys = lax.dynamic_slice_in_dim(keys_padded, tile_row, 11, 0).reshape(11 * TOK_DEV, HEADS, HD)
        near_values = lax.dynamic_slice_in_dim(values_padded, tile_row, 11, 0).reshape(11 * TOK_DEV, HEADS, HD)
        key_ids = (tile_row - 5) * QTILES + local_tiles
        listed = lax.dynamic_index_in_dim(windows, tile_row, 0, keepdims=False)
        allowed = jnp.any(listed[:, :, None] == key_ids[None, None, :], axis=1)
        allowed = jnp.broadcast_to(allowed[:, None, :, None], (QTILES, TILE, 11 * QTILES, TILE))
        allowed = allowed.reshape(TOK_DEV, 11 * TOK_DEV)
        own_queries = lax.dynamic_index_in_dim(queries, tile_row, 0, keepdims=False)
        score = jnp.einsum('qhd,khd->hqk', own_queries.astype(jnp.float32), near_keys.astype(jnp.float32)) * HD ** (-0.5)
        weight = jnp.where(allowed[None], jnp.exp(score), 0.0)
        totals = lax.optimization_barrier(jnp.sum(weight, axis=-1))
        rounded = lax.optimization_barrier(weight.astype(jnp.bfloat16)).astype(jnp.float32)
        gathered_sum = jnp.einsum('hqk,khd->qhd', rounded, near_values.astype(jnp.float32))
        return (gathered_sum / totals.T[:, :, None]).astype(jnp.bfloat16)
    attended = lax.map(attend, jnp.arange(SLABS, dtype=jnp.int32))
    attended = attended.reshape(TOKENS, HEADS * HD)
    rotated_heads = rotate_exact(attended.astype(jnp.float32) * signed(oin_sign)).astype(jnp.bfloat16)
    out_weight = levels(out_codes, out_scale, HEADS * HD)
    group_cols = HEADS * HD // N_HEAD
    summed = jnp.zeros((TOKENS, D), jnp.float32)
    for group in range(N_HEAD):
        group_term = jnp.dot(rotated_heads[:, group * group_cols:(group + 1) * group_cols], out_weight[group * group_cols:(group + 1) * group_cols], preferred_element_type=jnp.float32)
        summed = summed + lax.optimization_barrier(group_term.astype(jnp.bfloat16)).astype(jnp.float32)
    result_rows = (rotate_exact(summed) * signed(out_sign)).astype(jnp.bfloat16)
    return result_rows.reshape(SLABS, TOK_DEV, D)
```

```python
import functools

import jax
import jax.numpy as jnp
import numpy as np
from jax import lax
from jax.experimental import pallas as pl
from jax.experimental.pallas import tpu as pltpu
from jax.sharding import PartitionSpec as P

HD = 128
HAD = 128
TILE = 64
HROWS = 4
PLANES = 8
GROUP = HAD // PLANES
EPSILON = 1e-06
MESH = pl.DeviceIdType.MESH
VLIMIT = 60 * 1024 * 1024


def sylvester(order_size):
    matrix_now = np.ones((1, 1), np.float32)
    seed_pair = np.array([[1.0, 1.0], [1.0, -1.0]], np.float32)
    while matrix_now.shape[0] < order_size:
        matrix_now = np.kron(matrix_now, seed_pair)
    return matrix_now


ORDER = np.array([8 * i + k for k in range(PLANES) for i in range(GROUP)])
PLANE_POWER = np.array([4.0**k for k in range(PLANES) for _ in range(GROUP)], np.float32)


def plain_matrix():
    return jnp.asarray(sylvester(HAD), jnp.bfloat16)


def plane_matrix():
    return jnp.asarray(sylvester(HAD)[:, ORDER], jnp.bfloat16)


def plane_scale():
    return jnp.asarray((HAD**-0.5 / PLANE_POWER)[None, :], jnp.float32)


def plane_power():
    return jnp.asarray(PLANE_POWER[None, :], jnp.float32)


def signed(sign_bits):
    return (2 * sign_bits - 1).astype(jnp.float32)


def dot(left, right):
    return jnp.dot(left, right, preferred_element_type=jnp.float32)


def rotate_split(block, matrix):
    high = block.astype(jnp.bfloat16)
    low = (block - high.astype(jnp.float32)).astype(jnp.bfloat16)
    return (dot(high, matrix) + dot(low, matrix)) * HAD**-0.5


def unpack_block(words):
    planes = [(words & (3 << (2 * k))).astype(jnp.float32).astype(jnp.bfloat16) for k in range(PLANES)]
    pieces = []
    for block in range(words.shape[0] // GROUP):
        for k in range(PLANES):
            pieces.append(planes[k][block * GROUP : (block + 1) * GROUP])
    return jnp.concatenate(pieces, axis=0)


def row_sums(rows, power):
    total = None
    for block in range(rows.shape[1] // HAD):
        part = rows[:, block * HAD : (block + 1) * HAD].astype(jnp.float32) * power
        total = part if total is None else total + part
    return jnp.sum(total, axis=1, keepdims=True)


def gather_kernel(n, chunks, x_ref, sign_ref, mat_ref, scale_ref, out_ref, *sems):
    me = lax.axis_index("head")
    rows, width = x_ref.shape
    barrier = pltpu.get_barrier_semaphore()
    if n == 4:
        partner = me + 1 - 2 * (me % 2)
        across = (me + 2) % 4
        peers = [partner, across]
    else:
        peers = [(me + p) % n for p in range(1, n)]
    for peer in peers:
        pl.semaphore_signal(barrier, inc=1, device_id={"head": peer}, device_id_type=MESH)
    for block in range(width // HAD):
        cols = slice(block * HAD, (block + 1) * HAD)
        turned = dot(x_ref[:, cols] * sign_ref[:, cols].astype(jnp.bfloat16), mat_ref[...])
        out_ref[me, :, cols] = (turned * scale_ref[...]).astype(jnp.bfloat16)
    pl.semaphore_wait(barrier, len(peers))
    if n == 4:
        a_send, a_recv, f_send, f_recv, b_send, b_recv = sems
        step = rows // chunks

        def piece(slot, c):
            return out_ref.at[slot, pl.ds(c * step, step), :]

        crossing = [
            pltpu.make_async_remote_copy(
                piece(me, c), piece(me, c), a_send.at[c], a_recv.at[c],
                device_id={"head": across}, device_id_type=MESH,
            )
            for c in range(chunks)
        ]
        for copy in crossing:
            copy.start()
        beside = pltpu.make_async_remote_copy(
            out_ref.at[me], out_ref.at[me], b_send, b_recv,
            device_id={"head": partner}, device_id_type=MESH,
        )
        beside.start()
        relays = []
        for c in range(chunks):
            crossing[c].wait_recv()
            relay = pltpu.make_async_remote_copy(
                piece(across, c), piece(across, c), f_send.at[c], f_recv.at[c],
                device_id={"head": partner}, device_id_type=MESH,
            )
            relay.start()
            relays.append(relay)
        for copy in crossing:
            copy.wait_send()
        beside.wait()
        for copy in relays:
            copy.wait()
    else:
        send, recv = sems
        copies = [
            pltpu.make_async_remote_copy(
                out_ref.at[me], out_ref.at[me], send.at[p], recv.at[p],
                device_id={"head": peer}, device_id_type=MESH,
            )
            for p, peer in enumerate(peers)
        ]
        for copy in copies:
            copy.start()
        for copy in copies:
            copy.wait()


def gather_turned(own, sign_row, n):
    rows, width = own.shape
    chunks = 4
    if n == 4:
        sems = [pltpu.SemaphoreType.DMA((chunks,))] * 4 + [pltpu.SemaphoreType.DMA] * 2
    else:
        sems = [pltpu.SemaphoreType.DMA((n - 1,))] * 2
    return pl.pallas_call(
        functools.partial(gather_kernel, n, chunks),
        name="gather_turned",
        out_shape=jax.ShapeDtypeStruct((n, rows, width), jnp.bfloat16),
        in_specs=[pl.BlockSpec(memory_space=pltpu.VMEM)] * 4,
        out_specs=pl.BlockSpec(memory_space=pltpu.VMEM),
        scratch_shapes=sems,
        compiler_params=pltpu.CompilerParams(collective_id=0, has_side_effects=True),
    )(own, sign_row, plane_matrix(), plane_scale())


def project_kernel(per_part, cols, turned_ref, codes_ref, scale_ref, sign_ref, mat_ref, power_ref,
                   out_ref, words, offset, sems):
    step = pl.program_id(0)
    n, rows, width = turned_ref.shape
    count = 3 * per_part

    def fetch(index):
        part, place = index // per_part, index % per_part
        return pltpu.make_async_copy(
            codes_ref.at[part, :, pl.ds(pl.multiple_of(place * cols, HD), cols)],
            words.at[index],
            sems.at[index],
        )

    @pl.when(step == 0)
    def _():
        for index in range(count):
            fetch(index).start()
        total = jnp.zeros((rows, 1), jnp.float32)
        for shard in range(n):
            total = total + row_sums(turned_ref[shard], power_ref[...])
        offset[...] = jnp.broadcast_to(1.5 * total, offset.shape)

    fetch(step).wait()
    depth = width // PLANES
    result = jnp.zeros((rows, cols), jnp.float32)
    for shard in range(n):
        weights = unpack_block(words[step, shard * depth : (shard + 1) * depth, :])
        result = result + dot(turned_ref[shard], weights)
    for head in range(cols // HD):
        lanes = slice(head * HD, (head + 1) * HD)
        block = (result[:, lanes] - offset[...]) * scale_ref[:, lanes]
        block = rotate_split(block, mat_ref[...]) * sign_ref[:, lanes]
        mean = jnp.mean(block * block, axis=-1, keepdims=True)
        divisor = jnp.where(step < 2 * per_part, jnp.sqrt(mean + EPSILON), 1.0)
        out_ref[:, lanes] = (block / divisor).astype(jnp.bfloat16)


def project(turned, codes, scale_row, sign_row):
    n, rows, width = turned.shape
    _, inner, local = codes.shape
    cols = 256 if local % 256 == 0 else HD
    per_part = local // cols
    count = 3 * per_part
    return pl.pallas_call(
        functools.partial(project_kernel, per_part, cols),
        name="project",
        grid=(count,),
        out_shape=jax.ShapeDtypeStruct((rows, 3 * local), jnp.bfloat16),
        in_specs=[
            pl.BlockSpec((n, rows, width), lambda j: (0, 0, 0), pipeline_mode=pl.Buffered(1)),
            pl.BlockSpec(memory_space=pl.ANY),
            pl.BlockSpec((1, cols), lambda j: (0, j)),
            pl.BlockSpec((1, cols), lambda j: (0, j)),
            pl.BlockSpec((HAD, HAD), lambda j: (0, 0)),
            pl.BlockSpec((1, HAD), lambda j: (0, 0)),
        ],
        out_specs=pl.BlockSpec((rows, cols), lambda j: (0, j)),
        scratch_shapes=[
            pltpu.VMEM((count, inner, cols), jnp.int32),
            pltpu.VMEM((rows, HD), jnp.float32),
            pltpu.SemaphoreType.DMA((count,)),
        ],
        compiler_params=pltpu.CompilerParams(vmem_limit_bytes=VLIMIT),
    )(turned, codes, scale_row, sign_row, plain_matrix(), plane_power())


def halo_kernel(peers, distances, local, kv_ref, out_ref, send, recv):
    row = lax.axis_index("height")
    barrier = pltpu.get_barrier_semaphore()
    greeted = jnp.int32(0)
    for distance in distances:
        inside = jnp.logical_and(row + distance >= 0, row + distance < peers)

        @pl.when(inside)
        def _():
            pl.semaphore_signal(
                barrier, inc=1, device_id={"height": row + distance}, device_id_type=MESH
            )

        greeted = greeted + jnp.where(inside, 1, 0)

    pl.semaphore_wait(barrier, greeted)

    def copy_of(slot):
        return pltpu.make_async_remote_copy(
            kv_ref.at[:, pl.ds(local, 2 * local)], out_ref.at[slot], send.at[slot], recv.at[slot],
            device_id={"height": row + distances[slot]}, device_id_type=MESH,
        )

    for slot, distance in enumerate(distances):
        gives = jnp.logical_and(row + distance >= 0, row + distance < peers)
        takes = jnp.logical_and(row - distance >= 0, row - distance < peers)

        @pl.when(gives)
        def _():
            copy_of(slot).start()

        @pl.when(jnp.logical_not(takes))
        def _():
            out_ref[slot] = jnp.zeros(out_ref.shape[1:], out_ref.dtype)

    for slot, distance in enumerate(distances):
        gives = jnp.logical_and(row + distance >= 0, row + distance < peers)
        takes = jnp.logical_and(row - distance >= 0, row - distance < peers)

        @pl.when(gives)
        def _():
            copy_of(slot).wait_send()

        @pl.when(takes)
        def _():
            copy_of(slot).wait_recv()


def exchange_halo(qkv, peers, distances, local):
    rows = qkv.shape[0]
    slots = len(distances)
    return pl.pallas_call(
        functools.partial(halo_kernel, peers, distances, local),
        name="exchange_halo",
        out_shape=jax.ShapeDtypeStruct((slots, rows, 2 * local), jnp.bfloat16),
        in_specs=[pl.BlockSpec(memory_space=pltpu.VMEM)],
        out_specs=pl.BlockSpec(memory_space=pltpu.VMEM),
        scratch_shapes=[pltpu.SemaphoreType.DMA((slots,))] * 2,
        compiler_params=pltpu.CompilerParams(collective_id=1, has_side_effects=True),
    )(qkv)


def attend_kernel(distances, local, place_ref, listed_ref, qkv_ref, near_ref, osign_ref, mat_ref,
                  pscale_ref, power_ref, codes_ref, scale_ref, out_ref, rotated, offset):
    rows = qkv_ref.shape[0]
    qtiles = rows // TILE
    blocks = 1 + len(distances)

    @pl.when(pl.program_id(0) == 0)
    def _():
        keys = blocks * rows
        row = place_ref[0]
        lane = lax.broadcasted_iota(jnp.int32, (8, keys), 1) // TILE
        ids = lane + row * qtiles
        for slot, distance in enumerate(distances):
            first = (slot + 1) * qtiles
            shift = (row - distance) * qtiles - first
            inside = jnp.logical_and(lane >= first, lane < first + qtiles)
            ids = jnp.where(inside, lane + shift, ids)
        masks = []
        for tile in range(qtiles):
            hit = ids == listed_ref[tile, 0]
            for entry in range(1, listed_ref.shape[1]):
                hit = jnp.logical_or(hit, ids == listed_ref[tile, entry])
            line = jnp.where(hit, 1.0, 0.0)
            masks.extend([line] * (TILE // 8))
        mask = jnp.concatenate(masks, axis=0)
        for head in range(local // HD):
            own = [
                qkv_ref[:, part * local + head * HD : part * local + (head + 1) * HD]
                for part in range(3)
            ]
            lanes = slice(head * HD, (head + 1) * HD)
            later = slice(local + head * HD, local + (head + 1) * HD)
            near_keys = jnp.concatenate(
                [own[1]] + [near_ref[s, :, lanes] for s in range(blocks - 1)], axis=0
            )
            near_values = jnp.concatenate(
                [own[2]] + [near_ref[s, :, later] for s in range(blocks - 1)], axis=0
            )
            score = lax.dot_general(
                own[0], near_keys, (((1,), (1,)), ((), ())), preferred_element_type=jnp.float32
            )
            weight = jnp.exp(score * HD**-0.5) * mask
            totals = jnp.sum(weight, axis=-1, keepdims=True)
            gathered = dot(weight.astype(jnp.bfloat16), near_values)
            attended = (gathered / totals).astype(jnp.bfloat16)
            flipped = attended * osign_ref[:, lanes].astype(jnp.bfloat16)
            turned = dot(flipped, mat_ref[...]) * pscale_ref[...]
            rotated[:, lanes] = turned.astype(jnp.bfloat16)
        total = row_sums(rotated[...], power_ref[...])
        offset[...] = jnp.broadcast_to(1.5 * total, offset.shape)

    result = dot(rotated[...], unpack_block(codes_ref[...]))
    for part in range(result.shape[1] // HAD):
        lanes = slice(part * HAD, (part + 1) * HAD)
        out_ref[:, lanes] = ((result[:, lanes] - offset[...]) * scale_ref[:, lanes]).astype(jnp.bfloat16)


def attend_and_project(place, listed, qkv, near, osign_row, codes, scale_row, distances):
    rows = qkv.shape[0]
    local = qkv.shape[1] // 3
    features = codes.shape[1]
    cols = 512

    def fixed(shape):
        return pl.BlockSpec(shape, lambda j: (0,) * len(shape), pipeline_mode=pl.Buffered(1))

    return pl.pallas_call(
        functools.partial(attend_kernel, distances, local),
        name="attend_and_project",
        grid=(features // cols,),
        out_shape=jax.ShapeDtypeStruct((rows, features), jnp.bfloat16),
        in_specs=[
            pl.BlockSpec(memory_space=pltpu.SMEM),
            pl.BlockSpec(memory_space=pltpu.SMEM),
            fixed(qkv.shape),
            fixed(near.shape),
            fixed(osign_row.shape),
            fixed((HAD, HAD)),
            fixed((1, HAD)),
            fixed((1, HAD)),
            pl.BlockSpec((codes.shape[0], cols), lambda j: (0, j)),
            pl.BlockSpec((1, cols), lambda j: (0, j)),
        ],
        out_specs=pl.BlockSpec((rows, cols), lambda j: (0, j)),
        scratch_shapes=[
            pltpu.VMEM((rows, local), jnp.bfloat16),
            pltpu.VMEM((rows, HAD), jnp.float32),
        ],
        compiler_params=pltpu.CompilerParams(vmem_limit_bytes=VLIMIT),
    )(place, listed, qkv, near, osign_row, plane_matrix(), plane_scale(), plane_power(), codes, scale_row)


def scatter_kernel(n, chunks, part_ref, sign_ref, mat_ref, out_ref, *scratch):
    me = lax.axis_index("head")
    share, features = out_ref.shape
    barrier = pltpu.get_barrier_semaphore()
    if n == 4:
        partner = me + 1 - 2 * (me % 2)
        across = (me + 2) % 4
        diagonal = (partner + 2) % 4
        peers = [partner, across]
    else:
        peers = [(me + p) % n for p in range(1, n)]
    for peer in peers:
        pl.semaphore_signal(barrier, inc=1, device_id={"head": peer}, device_id_type=MESH)
    pl.semaphore_wait(barrier, len(peers))
    if n == 4:
        beside, staged, summed, crossed, a_send, a_recv, b_send, b_recv, x_send, x_recv = scratch
        step = share // chunks
        first = [
            pltpu.make_async_remote_copy(
                part_ref.at[diagonal, pl.ds(c * step, step), :],
                staged.at[pl.ds(c * step, step), :],
                a_send.at[c], a_recv.at[c],
                device_id={"head": partner}, device_id_type=MESH,
            )
            for c in range(chunks)
        ]
        for copy in first:
            copy.start()
        second = pltpu.make_async_remote_copy(
            part_ref.at[partner], beside, b_send, b_recv,
            device_id={"head": partner}, device_id_type=MESH,
        )
        second.start()
        third = []
        for c in range(chunks):
            first[c].wait_recv()
            rows = pl.ds(c * step, step)
            summed[rows, :] = (
                part_ref[across, rows, :].astype(jnp.float32) + staged[rows, :].astype(jnp.float32)
            ).astype(jnp.bfloat16)
            copy = pltpu.make_async_remote_copy(
                summed.at[rows, :], crossed.at[rows, :], x_send.at[c], x_recv.at[c],
                device_id={"head": across}, device_id_type=MESH,
            )
            copy.start()
            third.append(copy)
        for copy in first:
            copy.wait_send()
        second.wait()
        for copy in third:
            copy.wait()
        terms = [lambda cols: beside[:, cols], lambda cols: crossed[:, cols]]
    else:
        slots, send, recv = scratch
        copies = [
            pltpu.make_async_remote_copy(
                part_ref.at[peer], slots.at[p], send.at[p], recv.at[p],
                device_id={"head": peer}, device_id_type=MESH,
            )
            for p, peer in enumerate(peers)
        ]
        for copy in copies:
            copy.start()
        for copy in copies:
            copy.wait()
        terms = [functools.partial(lambda p, cols: slots[p, :, cols], p) for p in range(n - 1)]
    for block in range(features // HAD):
        cols = slice(block * HAD, (block + 1) * HAD)
        total = part_ref[me, :, cols].astype(jnp.float32)
        for term in terms:
            total = total + term(cols).astype(jnp.float32)
        out_ref[:, cols] = (rotate_split(total, mat_ref[...]) * sign_ref[:, cols]).astype(jnp.bfloat16)


def scatter_and_rotate(partial_rows, sign_row, n):
    rows, features = partial_rows.shape
    share = rows // n
    chunks = 3
    block = pltpu.VMEM((share, features), jnp.bfloat16)
    if n == 4:
        scratch = [block] * 4 + [
            pltpu.SemaphoreType.DMA((chunks,)), pltpu.SemaphoreType.DMA((chunks,)),
            pltpu.SemaphoreType.DMA, pltpu.SemaphoreType.DMA,
            pltpu.SemaphoreType.DMA((chunks,)), pltpu.SemaphoreType.DMA((chunks,)),
        ]
    else:
        scratch = [pltpu.VMEM((n - 1, share, features), jnp.bfloat16)] + [
            pltpu.SemaphoreType.DMA((n - 1,))
        ] * 2
    return pl.pallas_call(
        functools.partial(scatter_kernel, n, chunks),
        name="scatter_and_rotate",
        out_shape=jax.ShapeDtypeStruct((share, features), jnp.bfloat16),
        in_specs=[pl.BlockSpec(memory_space=pltpu.VMEM)] * 3,
        out_specs=pl.BlockSpec(memory_space=pltpu.VMEM),
        scratch_shapes=scratch,
        compiler_params=pltpu.CompilerParams(
            collective_id=2, has_side_effects=True, vmem_limit_bytes=VLIMIT
        ),
    )(partial_rows.reshape(n, share, features), sign_row, plain_matrix())


def on_device(
    n,
    peers,
    tokens,
    in_sign,
    qkv_codes,
    qkv_scale,
    qkv_sign,
    windows,
    oin_sign,
    out_codes,
    out_scale,
    out_sign,
):
    own = tokens[0]
    width = own.shape[1]
    model = width * n
    local = qkv_scale.shape[1]
    heads_width = local * n
    place = lax.axis_index("head")
    row_place = lax.axis_index("height").astype(jnp.int32)
    own_sign = lax.dynamic_slice_in_dim(in_sign, place * width, width, 0)
    turned = gather_turned(own, signed(own_sign)[None], n)
    qkv = project(
        turned,
        jnp.transpose(qkv_codes, (1, 0, 2)),
        (qkv_scale * model**-0.5).reshape(1, 3 * local),
        signed(qkv_sign).reshape(1, 3 * local),
    )
    reach = (1,) if peers <= HROWS else (1, HROWS - 1, HROWS, HROWS + 1)
    distances = tuple(d for r in reach if r < peers for d in (r, -r))
    near = exchange_halo(qkv, peers, distances, local)
    partial_rows = attend_and_project(
        row_place[None],
        windows[0],
        qkv,
        near,
        signed(oin_sign)[None],
        out_codes,
        (out_scale * heads_width**-0.5)[None],
        distances,
    )
    return scatter_and_rotate(partial_rows, signed(out_sign)[None], n)[None]


def solution(mesh):
    n = mesh.shape["head"]
    peers = mesh.shape["height"]
    return jax.shard_map(
        functools.partial(on_device, n, peers),
        mesh=mesh,
        in_specs=(
            P(("clip", "height"), None, "head"),
            P(),
            P(None, None, "head"),
            P(None, "head"),
            P(None, "head"),
            P(("clip", "height"), None, None),
            P("head"),
            P("head", None),
            P(),
            P(),
        ),
        out_specs=P(("clip", "height"), "head", None),
        check_vma=False,
    )
```

```python
import functools

import jax
import jax.numpy as jnp
import numpy as np
from jax import lax
from jax.experimental import pallas as pl
from jax.experimental.pallas import tpu as pltpu
from jax.sharding import PartitionSpec as P

HD = 128
HAD = 128
TILE = 64
HROWS = 4
PLANES = 8
GROUP = HAD // PLANES
EPSILON = 1e-06
MESH = pl.DeviceIdType.MESH
VLIMIT = 60 * 1024 * 1024


def sylvester(order_size):
    matrix_now = np.ones((1, 1), np.float32)
    seed_pair = np.array([[1.0, 1.0], [1.0, -1.0]], np.float32)
    while matrix_now.shape[0] < order_size:
        matrix_now = np.kron(matrix_now, seed_pair)
    return matrix_now


ORDER = np.array([8 * i + k for k in range(PLANES) for i in range(GROUP)])
PLANE_POWER = np.array([4.0**k for k in range(PLANES) for _ in range(GROUP)], np.float32)


def plain_matrix():
    return jnp.asarray(sylvester(HAD), jnp.bfloat16)


def plane_matrix():
    return jnp.asarray(sylvester(HAD)[:, ORDER], jnp.bfloat16)


def plane_scale():
    return jnp.asarray((HAD**-0.5 / PLANE_POWER)[None, :], jnp.float32)


def plane_power():
    return jnp.asarray(PLANE_POWER[None, :], jnp.float32)


def signed(sign_bits):
    return (2 * sign_bits - 1).astype(jnp.float32)


def dot(left, right):
    return jnp.dot(left, right, preferred_element_type=jnp.float32)


def rotate_split(block, matrix):
    high = block.astype(jnp.bfloat16)
    low = (block - high.astype(jnp.float32)).astype(jnp.bfloat16)
    return (dot(high, matrix) + dot(low, matrix)) * HAD**-0.5


def unpack_block(words):
    planes = [(words & (3 << (2 * k))).astype(jnp.float32).astype(jnp.bfloat16) for k in range(PLANES)]
    pieces = []
    for block in range(words.shape[0] // GROUP):
        for k in range(PLANES):
            pieces.append(planes[k][block * GROUP : (block + 1) * GROUP])
    return jnp.concatenate(pieces, axis=0)


def row_sums(rows, power):
    total = None
    for block in range(rows.shape[1] // HAD):
        part = rows[:, block * HAD : (block + 1) * HAD].astype(jnp.float32) * power
        total = part if total is None else total + part
    return jnp.sum(total, axis=1, keepdims=True)


def layer_kernel(
    n, peers, distances, cols, gcols,
    x_ref, insign_ref, qscale_ref, qsign_ref, listed_ref, osign_ref, oscale_ref, outsign_ref,
    plane_mat_ref, mat_ref, pscale_ref, power_ref, codes_ref, ocodes_ref,
    out_ref,
    turned, words, weights, acc, offset, qkv, near, owords, oweights, gathered, totals,
    rotated, ooffset, lines, part, word_sem, oword_sem, halo_send, halo_recv, *scratch,
):
    me = lax.axis_index("head")
    row = lax.axis_index("height")
    rows, width = x_ref.shape
    count = words.shape[0]
    per_part = count // 3
    per_chunk = cols // HD
    local = per_part * cols
    depth = width // PLANES
    qtiles = rows // TILE
    groups = part.shape[0]
    share = rows // n
    slots = len(distances)

    def fetch(j):
        return pltpu.make_async_copy(
            codes_ref.at[(j // per_part + 1) % 3, :, pl.ds(pl.multiple_of(j % per_part * cols, HD), cols)],
            words.at[j],
            word_sem.at[j],
        )

    for j in range(count):
        fetch(j).start()
    fetch_out = pltpu.make_async_copy(ocodes_ref, owords, oword_sem)
    fetch_out.start()

    barrier = pltpu.get_barrier_semaphore()
    if n == 4:
        partner = me + 1 - 2 * (me % 2)
        across = (me + 2) % 4
        diagonal = (partner + 2) % 4
        head_peers = [partner, across]
        early, late = [me, partner], [across, diagonal]
    else:
        head_peers = [(me + p) % n for p in range(1, n)]
        early, late = [me], head_peers
    gives = [jnp.logical_and(row + d >= 0, row + d < peers) for d in distances]
    takes = [jnp.logical_and(row - d >= 0, row - d < peers) for d in distances]
    for peer in head_peers:
        pl.semaphore_signal(barrier, inc=1, device_id={"head": peer}, device_id_type=MESH)
    greeted = jnp.int32(len(head_peers))
    for slot, distance in enumerate(distances):

        @pl.when(gives[slot])
        def _():
            pl.semaphore_signal(
                barrier, inc=1, device_id={"height": row + distance}, device_id_type=MESH
            )

        greeted = greeted + jnp.where(gives[slot], 1, 0)

    for block in range(width // HAD):
        lanes = slice(block * HAD, (block + 1) * HAD)
        spun = dot(x_ref[:, lanes] * insign_ref[:, lanes].astype(jnp.bfloat16), plane_mat_ref[...])
        turned[me, :, lanes] = (spun * pscale_ref[...]).astype(jnp.bfloat16)
    for j in range(count):
        source = (j // per_part + 1) % 3
        spots = slice(j % per_part * cols, (j % per_part + 1) * cols)
        for place, ref in enumerate((qscale_ref, qsign_ref)):
            line = jnp.broadcast_to(ref[source : source + 1, spots], (8, cols))
            lines[j, 8 * place : 8 * place + 8, :] = line
    pl.semaphore_wait(barrier, greeted)

    def head_copy(src, dst, send, recv, peer):
        return pltpu.make_async_remote_copy(
            src, dst, send, recv, device_id={"head": peer}, device_id_type=MESH
        )

    def unpack(j):
        fetch(j).wait()
        for shard in range(n):
            weights[j, shard] = unpack_block(words[j, shard * depth : (shard + 1) * depth, :])
        total = dot(turned[early[0]], weights[j, early[0]])
        for shard in early[1:]:
            total = total + dot(turned[shard], weights[j, shard])
        acc[j] = total

    if n == 4:
        a_send, a_recv, f_send, f_recv, b_send, b_recv = scratch[:6]
        scratch = scratch[6:]
        chunks = a_send.shape[0]
        step = rows // chunks

        def piece(slot, c):
            return turned.at[slot, pl.ds(c * step, step), :]

        crossing = [
            head_copy(piece(me, c), piece(me, c), a_send.at[c], a_recv.at[c], across)
            for c in range(chunks)
        ]
        relays = [
            head_copy(piece(across, c), piece(across, c), f_send.at[c], f_recv.at[c], partner)
            for c in range(chunks)
        ]
        for copy in crossing:
            copy.start()
        beside = head_copy(turned.at[me], turned.at[me], b_send, b_recv, partner)
        beside.start()
        beside.wait_recv()
        done = 0
        for c in range(chunks):
            upto = count * (c + 1) // chunks

            @pl.loop(done, upto)
            def _(j):
                unpack(j)

            done = upto
            crossing[c].wait_recv()
            relays[c].start()
        for copy in relays:
            copy.wait_recv()
        sent = crossing + relays + [beside]
    else:
        g_send, g_recv = scratch[:2]
        scratch = scratch[2:]
        sent = [
            head_copy(turned.at[me], turned.at[me], g_send.at[p], g_recv.at[p], peer)
            for p, peer in enumerate(head_peers)
        ]
        for copy in sent:
            copy.start()

        @pl.loop(0, count)
        def _(j):
            unpack(j)

        for copy in sent:
            copy.wait_recv()

    total = jnp.zeros((rows, 1), jnp.float32)
    for shard in range(n):
        total = total + row_sums(turned[shard], power_ref[...])
    offset[...] = jnp.broadcast_to(1.5 * total, offset.shape)

    def finish(j):
        result = acc[j]
        for shard in late:
            result = result + dot(turned[shard], weights[j, shard])
        source = (j // per_part + 1) % 3
        for head in range(per_chunk):
            lanes = slice(head * HD, (head + 1) * HD)
            block = (result[:, lanes] - offset[...]) * lines[j, 0:1, lanes]
            block = rotate_split(block, mat_ref[...]) * lines[j, 8:9, lanes]
            mean = jnp.mean(block * block, axis=-1, keepdims=True)
            divisor = jnp.where(source < 2, jnp.sqrt(mean + EPSILON), 1.0)
            qkv[j, :, lanes] = (block / divisor).astype(jnp.bfloat16)

    def halo_copy(slot, j):
        return pltpu.make_async_remote_copy(
            qkv.at[j], near.at[slot, j], halo_send.at[slot, j], halo_recv.at[slot, j],
            device_id={"height": row + distances[slot]}, device_id_type=MESH,
        )

    @pl.loop(0, 2 * per_part)
    def _(j):
        finish(j)
        for slot in range(slots):

            @pl.when(gives[slot])
            def _():
                halo_copy(slot, j).start()

    for slot in range(slots):

        @pl.when(jnp.logical_not(takes[slot]))
        def _():
            near[slot] = jnp.zeros(near.shape[1:], near.dtype)

    @pl.loop(2 * per_part, count)
    def _(j):
        finish(j)

    def mask_of(first_tile):
        ids = lax.broadcasted_iota(jnp.int32, (8, rows), 1) // TILE + first_tile
        stack = []
        for tile in range(qtiles):
            hit = ids == listed_ref[0, tile, 0]
            for entry in range(1, listed_ref.shape[2]):
                hit = jnp.logical_or(hit, ids == listed_ref[0, tile, entry])
            stack.extend([jnp.where(hit, 1.0, 0.0)] * (TILE // 8))
        return jnp.concatenate(stack, axis=0)

    def attend(queries, keys, values, mask):
        score = lax.dot_general(
            queries, keys, (((1,), (1,)), ((), ())), preferred_element_type=jnp.float32
        )
        weight = jnp.exp(score * HD**-0.5) * mask
        return dot(weight.astype(jnp.bfloat16), values), jnp.sum(weight, axis=-1, keepdims=True)

    own_mask = mask_of(row * qtiles)
    near_masks = [mask_of((row - d) * qtiles) for d in distances]
    for head in range(local // HD):
        chunk, lanes = head // per_chunk, slice(head % per_chunk * HD, (head % per_chunk + 1) * HD)
        found, sums = attend(
            qkv[2 * per_part + chunk, :, lanes], qkv[chunk, :, lanes],
            qkv[per_part + chunk, :, lanes], own_mask,
        )
        gathered[head] = found
        totals[head] = jnp.broadcast_to(sums, found.shape)

    fetch_out.wait()

    @pl.loop(0, groups)
    def _(g):
        spots = pl.ds(pl.multiple_of(g * gcols, HD), gcols)
        oweights[g] = unpack_block(owords[:, spots])

    for slot in range(slots):

        @pl.when(takes[slot])
        def _():
            for j in range(2 * per_part):
                halo_copy(slot, j).wait_recv()

    for head in range(local // HD):
        chunk, lanes = head // per_chunk, slice(head % per_chunk * HD, (head % per_chunk + 1) * HD)
        found, sums = gathered[head], totals[head]
        for slot in range(slots):
            more, more_sums = attend(
                qkv[2 * per_part + chunk, :, lanes], near[slot, chunk, :, lanes],
                near[slot, per_part + chunk, :, lanes], near_masks[slot],
            )
            found, sums = found + more, sums + more_sums
        attended = (found / sums).astype(jnp.bfloat16)
        spots = slice(head * HD, (head + 1) * HD)
        spun = dot(attended * osign_ref[:, spots].astype(jnp.bfloat16), plane_mat_ref[...])
        rotated[:, spots] = (spun * pscale_ref[...]).astype(jnp.bfloat16)
    ooffset[...] = jnp.broadcast_to(1.5 * row_sums(rotated[...], power_ref[...]), ooffset.shape)

    def produce(g):
        result = dot(rotated[...], oweights[g])
        for block in range(gcols // HAD):
            lanes = slice(block * HAD, (block + 1) * HAD)
            spots = slice(g * gcols + block * HAD, g * gcols + (block + 1) * HAD)
            value = (result[:, lanes] - ooffset[...]) * oscale_ref[:, spots]
            part[g, :, :, lanes] = value.reshape(n, share, HAD).astype(jnp.bfloat16)

    def conclude(g, terms):
        for block in range(gcols // HAD):
            lanes = slice(block * HAD, (block + 1) * HAD)
            spots = slice(g * gcols + block * HAD, g * gcols + (block + 1) * HAD)
            total = part[g, me, :, lanes].astype(jnp.float32)
            for term in terms:
                total = total + term[:, lanes].astype(jnp.float32)
            spun = rotate_split(total, mat_ref[...]) * outsign_ref[:, spots]
            out_ref[:, spots] = spun.astype(jnp.bfloat16)

    if n == 4:
        staged, flank, summed, crossed, p_send, p_recv, q_send, q_recv, x_send, x_recv = scratch
        first = [
            head_copy(part.at[g, diagonal], staged.at[g], p_send.at[g], p_recv.at[g], partner)
            for g in range(groups)
        ]
        second = [
            head_copy(part.at[g, partner], flank.at[g], q_send.at[g], q_recv.at[g], partner)
            for g in range(groups)
        ]
        third = [
            head_copy(summed.at[g], crossed.at[g], x_send.at[g], x_recv.at[g], across)
            for g in range(groups)
        ]

        def relay(g):
            first[g].wait_recv()
            summed[g] = (
                part[g, across].astype(jnp.float32) + staged[g].astype(jnp.float32)
            ).astype(jnp.bfloat16)
            third[g].start()

        for g in range(groups):
            produce(g)
            first[g].start()
            second[g].start()
            if g > 0:
                relay(g - 1)
        relay(groups - 1)
        for g in range(groups):
            second[g].wait_recv()
            third[g].wait_recv()
            conclude(g, [flank[g], crossed[g]])
        sent = sent + first + second + third
    else:
        landed, r_send, r_recv = scratch
        moves = []
        for g in range(groups):
            produce(g)
            move = [
                head_copy(part.at[g, peer], landed.at[p, g], r_send.at[p, g], r_recv.at[p, g], peer)
                for p, peer in enumerate(head_peers)
            ]
            for copy in move:
                copy.start()
            moves.append(move)
        for g in range(groups):
            for copy in moves[g]:
                copy.wait_recv()
            conclude(g, [landed[p, g] for p in range(n - 1)])
        sent = sent + [copy for move in moves for copy in move]

    for copy in sent:
        copy.wait_send()
    for slot in range(slots):

        @pl.when(gives[slot])
        def _():
            for j in range(2 * per_part):
                halo_copy(slot, j).wait_send()


def on_device(
    n,
    peers,
    tokens,
    in_sign,
    qkv_codes,
    qkv_scale,
    qkv_sign,
    windows,
    oin_sign,
    out_codes,
    out_scale,
    out_sign,
):
    own = tokens[0]
    rows, width = own.shape
    model = width * n
    local = qkv_scale.shape[1]
    features = out_codes.shape[1]
    place = lax.axis_index("head")
    own_sign = lax.dynamic_slice_in_dim(in_sign, place * width, width, 0)
    reach = (1,) if peers <= HROWS else (1, HROWS - 1, HROWS, HROWS + 1)
    distances = tuple(d for r in reach if r < peers for d in (r, -r))
    slots = len(distances)
    cols = 256 if local % 256 == 0 else HD
    count = 3 * local // cols
    per_part = count // 3
    inner = qkv_codes.shape[0]
    gcols = 1024 if features % 1024 == 0 else HD
    groups = features // gcols
    share = rows // n
    chunks = 4
    dma = pltpu.SemaphoreType.DMA
    grouped = pltpu.VMEM((groups, share, gcols), jnp.bfloat16)
    if n == 4:
        tail = [dma((chunks,))] * 4 + [dma] * 2 + [grouped] * 4 + [dma((groups,))] * 6
    else:
        tail = [dma((n - 1,))] * 2
        tail += [pltpu.VMEM((n - 1, groups, share, gcols), jnp.bfloat16)]
        tail += [dma((n - 1, groups))] * 2
    vmem = pl.BlockSpec(memory_space=pltpu.VMEM)
    anywhere = pl.BlockSpec(memory_space=pl.ANY)
    smem = pl.BlockSpec(memory_space=pltpu.SMEM)
    result = pl.pallas_call(
        functools.partial(layer_kernel, n, peers, distances, cols, gcols),
        name="layer",
        out_shape=jax.ShapeDtypeStruct((share, features), jnp.bfloat16),
        in_specs=[vmem] * 4 + [smem] + [vmem] * 7 + [anywhere] * 2,
        out_specs=vmem,
        scratch_shapes=[
            pltpu.VMEM((n, rows, width), jnp.bfloat16),
            pltpu.VMEM((count, inner, cols), jnp.int32),
            pltpu.VMEM((count, n, width, cols), jnp.bfloat16),
            pltpu.VMEM((count, rows, cols), jnp.float32),
            pltpu.VMEM((rows, HD), jnp.float32),
            pltpu.VMEM((count, rows, cols), jnp.bfloat16),
            pltpu.VMEM((slots, 2 * per_part, rows, cols), jnp.bfloat16),
            pltpu.VMEM(out_codes.shape, jnp.int32),
            pltpu.VMEM((groups, local, gcols), jnp.bfloat16),
            pltpu.VMEM((local // HD, rows, HD), jnp.float32),
            pltpu.VMEM((local // HD, rows, HD), jnp.float32),
            pltpu.VMEM((rows, local), jnp.bfloat16),
            pltpu.VMEM((rows, HD), jnp.float32),
            pltpu.VMEM((count, 16, cols), jnp.float32),
            pltpu.VMEM((groups, n, share, gcols), jnp.bfloat16),
            dma((count,)),
            dma,
            dma((slots, 2 * per_part)),
            dma((slots, 2 * per_part)),
        ]
        + tail,
        compiler_params=pltpu.CompilerParams(
            collective_id=0, has_side_effects=True, vmem_limit_bytes=VLIMIT
        ),
    )(
        own,
        signed(own_sign)[None],
        qkv_scale * model**-0.5,
        signed(qkv_sign),
        windows,
        signed(oin_sign)[None],
        (out_scale * (local * n) ** -0.5)[None],
        signed(out_sign)[None],
        plane_matrix(),
        plain_matrix(),
        plane_scale(),
        plane_power(),
        jnp.transpose(qkv_codes, (1, 0, 2)),
        out_codes,
    )
    return result[None]


def solution(mesh):
    n = mesh.shape["head"]
    peers = mesh.shape["height"]
    return jax.shard_map(
        functools.partial(on_device, n, peers),
        mesh=mesh,
        in_specs=(
            P(("clip", "height"), None, "head"),
            P(),
            P(None, None, "head"),
            P(None, "head"),
            P(None, "head"),
            P(("clip", "height"), None, None),
            P("head"),
            P("head", None),
            P(),
            P(),
        ),
        out_specs=P(("clip", "height"), "head", None),
        check_vma=False,
    )
```

```python
import functools

import jax
import jax.numpy as jnp
import numpy as np
from jax import lax
from jax.experimental import pallas as pl
from jax.experimental.pallas import tpu as pltpu
from jax.sharding import PartitionSpec as P

HD = 128
HAD = 128
TILE = 64
HROWS = 4
PLANES = 8
GROUP = HAD // PLANES
EPSILON = 1e-06
MESH = pl.DeviceIdType.MESH
VLIMIT = 60 * 1024 * 1024


def sylvester(order_size):
    matrix_now = np.ones((1, 1), np.float32)
    seed_pair = np.array([[1.0, 1.0], [1.0, -1.0]], np.float32)
    while matrix_now.shape[0] < order_size:
        matrix_now = np.kron(matrix_now, seed_pair)
    return matrix_now


ORDER = np.array([8 * i + k for k in range(PLANES) for i in range(GROUP)])
PLANE_POWER = np.array([4.0**k for k in range(PLANES) for _ in range(GROUP)], np.float32)


def plain_matrix():
    return jnp.asarray(sylvester(HAD), jnp.bfloat16)


def plane_matrix():
    return jnp.asarray(sylvester(HAD)[:, ORDER], jnp.bfloat16)


def plane_scale():
    return jnp.asarray((HAD**-0.5 / PLANE_POWER)[None, :], jnp.float32)


def plane_power():
    return jnp.asarray(PLANE_POWER[None, :], jnp.float32)


def signed(sign_bits):
    return (2 * sign_bits - 1).astype(jnp.float32)


def dot(left, right):
    return jnp.dot(left, right, preferred_element_type=jnp.float32)


def rotate_split(block, matrix):
    high = block.astype(jnp.bfloat16)
    low = (block - high.astype(jnp.float32)).astype(jnp.bfloat16)
    return (dot(high, matrix) + dot(low, matrix)) * HAD**-0.5


def unpack_block(words):
    planes = [(words & (3 << (2 * k))).astype(jnp.float32).astype(jnp.bfloat16) for k in range(PLANES)]
    pieces = []
    for block in range(words.shape[0] // GROUP):
        for k in range(PLANES):
            pieces.append(planes[k][block * GROUP : (block + 1) * GROUP])
    return jnp.concatenate(pieces, axis=0)


def row_sums(rows, power):
    total = None
    for block in range(rows.shape[1] // HAD):
        part = rows[:, block * HAD : (block + 1) * HAD].astype(jnp.float32) * power
        total = part if total is None else total + part
    return jnp.sum(total, axis=1, keepdims=True)


def layer_kernel(
    n, peers, distances, cols, gcols,
    x_ref, insigns_ref, qscale_ref, qsign_ref, listed_ref, osign_ref, oscale_ref, outsign_ref,
    plane_mat_ref, mat_ref, pscale_ref, power_ref, codes_ref, ocodes_ref,
    out_ref,
    turned, words, weights, acc, offset, qkv, near, owords, oweights, gathered, totals,
    rotated, ooffset, lines, insigns, part, word_sem, oword_sem, halo_send, halo_recv, *scratch,
):
    me = lax.axis_index("head")
    row = lax.axis_index("height")
    rows, width = x_ref.shape
    count = words.shape[0]
    per_part = count // 3
    per_chunk = cols // HD
    local = per_part * cols
    depth = width // PLANES
    qtiles = rows // TILE
    groups = part.shape[0]
    share = rows // n
    slots = len(distances)

    def fetch(j):
        return pltpu.make_async_copy(
            codes_ref.at[(j // per_part + 1) % 3, :, pl.ds(pl.multiple_of(j % per_part * cols, HD), cols)],
            words.at[j],
            word_sem.at[j],
        )

    for j in range(count):
        fetch(j).start()
    fetch_out = pltpu.make_async_copy(ocodes_ref, owords, oword_sem)
    fetch_out.start()

    barrier = pltpu.get_barrier_semaphore()
    if n == 4:
        partner = me + 1 - 2 * (me % 2)
        across = (me + 2) % 4
        diagonal = (partner + 2) % 4
        head_peers = [partner, across]
        early, late = [me, partner], [across, diagonal]
    else:
        head_peers = [(me + p) % n for p in range(1, n)]
        early, late = [me], head_peers
    gives = [jnp.logical_and(row + d >= 0, row + d < peers) for d in distances]
    takes = [jnp.logical_and(row - d >= 0, row - d < peers) for d in distances]
    for peer in head_peers:
        pl.semaphore_signal(barrier, inc=1, device_id={"head": peer}, device_id_type=MESH)
    greeted = jnp.int32(len(head_peers))
    for slot, distance in enumerate(distances):

        @pl.when(gives[slot])
        def _():
            pl.semaphore_signal(
                barrier, inc=1, device_id={"height": row + distance}, device_id_type=MESH
            )

        greeted = greeted + jnp.where(gives[slot], 1, 0)

    for shard in range(n):
        for block in range(width // HAD):
            lanes = slice(block * HAD, (block + 1) * HAD)
            line = signed(insigns_ref[shard * width + block * HAD : shard * width + (block + 1) * HAD])
            insigns[shard, :, lanes] = jnp.broadcast_to(line[None, :], (8, HAD))
    for block in range(width // HAD):
        lanes = slice(block * HAD, (block + 1) * HAD)
        spun = dot(x_ref[:, lanes] * insigns[me, 0:1, lanes].astype(jnp.bfloat16), plane_mat_ref[...])
        turned[me, :, lanes] = (spun * pscale_ref[...]).astype(jnp.bfloat16)
    for j in range(count):
        source = (j // per_part + 1) % 3
        spots = slice(j % per_part * cols, (j % per_part + 1) * cols)
        scale = qscale_ref[source : source + 1, spots] * (width * n) ** -0.5
        sign = signed(qsign_ref[source : source + 1, spots])
        lines[j, 0:8, :] = jnp.broadcast_to(scale, (8, cols))
        lines[j, 8:16, :] = jnp.broadcast_to(sign, (8, cols))
    pl.semaphore_wait(barrier, greeted)

    def head_copy(src, dst, send, recv, peer):
        return pltpu.make_async_remote_copy(
            src, dst, send, recv, device_id={"head": peer}, device_id_type=MESH
        )

    def unpack(j):
        fetch(j).wait()
        for shard in range(n):
            weights[j, shard] = unpack_block(words[j, shard * depth : (shard + 1) * depth, :])
        total = dot(turned[early[0]], weights[j, early[0]])
        for shard in early[1:]:
            total = total + dot(turned[shard], weights[j, shard])
        acc[j] = total

    if n == 4:
        a_send, a_recv, f_send, f_recv, b_send, b_recv = scratch[:6]
        scratch = scratch[6:]
        chunks = a_send.shape[0]
        step = rows // chunks

        def piece(slot, c):
            return turned.at[slot, pl.ds(c * step, step), :]

        crossing = [
            head_copy(piece(me, c), piece(me, c), a_send.at[c], a_recv.at[c], across)
            for c in range(chunks)
        ]
        relays = [
            head_copy(piece(across, c), piece(across, c), f_send.at[c], f_recv.at[c], partner)
            for c in range(chunks)
        ]
        for copy in crossing:
            copy.start()
        beside = head_copy(turned.at[me], turned.at[me], b_send, b_recv, partner)
        beside.start()
        beside.wait_recv()
        done = 0
        for c in range(chunks):
            upto = count * (c + 1) // chunks

            @pl.loop(done, upto)
            def _(j):
                unpack(j)

            done = upto
            crossing[c].wait_recv()
            relays[c].start()
        for copy in relays:
            copy.wait_recv()
        sent = crossing + relays + [beside]
    else:
        g_send, g_recv = scratch[:2]
        scratch = scratch[2:]
        sent = [
            head_copy(turned.at[me], turned.at[me], g_send.at[p], g_recv.at[p], peer)
            for p, peer in enumerate(head_peers)
        ]
        for copy in sent:
            copy.start()

        @pl.loop(0, count)
        def _(j):
            unpack(j)

        for copy in sent:
            copy.wait_recv()

    total = jnp.zeros((rows, 1), jnp.float32)
    for shard in range(n):
        total = total + row_sums(turned[shard], power_ref[...])
    offset[...] = jnp.broadcast_to(1.5 * total, offset.shape)

    def finish(j):
        result = acc[j]
        for shard in late:
            result = result + dot(turned[shard], weights[j, shard])
        source = (j // per_part + 1) % 3
        for head in range(per_chunk):
            lanes = slice(head * HD, (head + 1) * HD)
            block = (result[:, lanes] - offset[...]) * lines[j, 0:1, lanes]
            block = rotate_split(block, mat_ref[...]) * lines[j, 8:9, lanes]
            mean = jnp.mean(block * block, axis=-1, keepdims=True)
            divisor = jnp.where(source < 2, jnp.sqrt(mean + EPSILON), 1.0)
            qkv[j, :, lanes] = (block / divisor).astype(jnp.bfloat16)

    def halo_copy(slot, j):
        return pltpu.make_async_remote_copy(
            qkv.at[j], near.at[slot, j], halo_send.at[slot, j], halo_recv.at[slot, j],
            device_id={"height": row + distances[slot]}, device_id_type=MESH,
        )

    @pl.loop(0, 2 * per_part)
    def _(j):
        finish(j)
        for slot in range(slots):

            @pl.when(gives[slot])
            def _():
                halo_copy(slot, j).start()

    for slot in range(slots):

        @pl.when(jnp.logical_not(takes[slot]))
        def _():
            near[slot] = jnp.zeros(near.shape[1:], near.dtype)

    @pl.loop(2 * per_part, count)
    def _(j):
        finish(j)

    def mask_of(first_tile):
        ids = lax.broadcasted_iota(jnp.int32, (8, rows), 1) // TILE + first_tile
        stack = []
        for tile in range(qtiles):
            hit = ids == listed_ref[tile, 0, 0]
            for entry in range(1, listed_ref.shape[2]):
                hit = jnp.logical_or(hit, ids == listed_ref[tile, 0, entry])
            stack.extend([jnp.where(hit, 1.0, 0.0)] * (TILE // 8))
        return jnp.concatenate(stack, axis=0)

    def attend(queries, keys, values, mask):
        score = lax.dot_general(
            queries, keys, (((1,), (1,)), ((), ())), preferred_element_type=jnp.float32
        )
        weight = jnp.exp(score * HD**-0.5) * mask
        return dot(weight.astype(jnp.bfloat16), values), jnp.sum(weight, axis=-1, keepdims=True)

    own_mask = mask_of(row * qtiles)
    near_masks = [mask_of((row - d) * qtiles) for d in distances]
    for head in range(local // HD):
        chunk, lanes = head // per_chunk, slice(head % per_chunk * HD, (head % per_chunk + 1) * HD)
        found, sums = attend(
            qkv[2 * per_part + chunk, :, lanes], qkv[chunk, :, lanes],
            qkv[per_part + chunk, :, lanes], own_mask,
        )
        gathered[head] = found
        totals[head] = jnp.broadcast_to(sums, found.shape)

    fetch_out.wait()

    @pl.loop(0, groups)
    def _(g):
        spots = pl.ds(pl.multiple_of(g * gcols, HD), gcols)
        oweights[g] = unpack_block(owords[:, spots])

    for slot in range(slots):

        @pl.when(takes[slot])
        def _():
            for j in range(2 * per_part):
                halo_copy(slot, j).wait_recv()

    for head in range(local // HD):
        chunk, lanes = head // per_chunk, slice(head % per_chunk * HD, (head % per_chunk + 1) * HD)
        found, sums = gathered[head], totals[head]
        for slot in range(slots):
            more, more_sums = attend(
                qkv[2 * per_part + chunk, :, lanes], near[slot, chunk, :, lanes],
                near[slot, per_part + chunk, :, lanes], near_masks[slot],
            )
            found, sums = found + more, sums + more_sums
        attended = (found / sums).astype(jnp.bfloat16)
        spots = slice(head * HD, (head + 1) * HD)
        spun = dot(attended * signed(osign_ref[spots])[None, :].astype(jnp.bfloat16), plane_mat_ref[...])
        rotated[:, spots] = (spun * pscale_ref[...]).astype(jnp.bfloat16)
    ooffset[...] = jnp.broadcast_to(1.5 * row_sums(rotated[...], power_ref[...]), ooffset.shape)

    def produce(g):
        result = dot(rotated[...], oweights[g])
        for block in range(gcols // HAD):
            lanes = slice(block * HAD, (block + 1) * HAD)
            spots = slice(g * gcols + block * HAD, g * gcols + (block + 1) * HAD)
            value = (result[:, lanes] - ooffset[...]) * (oscale_ref[spots] * (local * n) ** -0.5)[None, :]
            part[g, :, :, lanes] = value.reshape(n, share, HAD).astype(jnp.bfloat16)

    def conclude(g, terms):
        for block in range(gcols // HAD):
            lanes = slice(block * HAD, (block + 1) * HAD)
            spots = slice(g * gcols + block * HAD, g * gcols + (block + 1) * HAD)
            total = part[g, me, :, lanes].astype(jnp.float32)
            for term in terms:
                total = total + term[:, lanes].astype(jnp.float32)
            spun = rotate_split(total, mat_ref[...]) * signed(outsign_ref[spots])[None, :]
            out_ref[:, spots] = spun.astype(jnp.bfloat16)

    if n == 4:
        staged, flank, summed, crossed, p_send, p_recv, q_send, q_recv, x_send, x_recv = scratch
        first = [
            head_copy(part.at[g, diagonal], staged.at[g], p_send.at[g], p_recv.at[g], partner)
            for g in range(groups)
        ]
        second = [
            head_copy(part.at[g, partner], flank.at[g], q_send.at[g], q_recv.at[g], partner)
            for g in range(groups)
        ]
        third = [
            head_copy(summed.at[g], crossed.at[g], x_send.at[g], x_recv.at[g], across)
            for g in range(groups)
        ]

        def relay(g):
            first[g].wait_recv()
            summed[g] = (
                part[g, across].astype(jnp.float32) + staged[g].astype(jnp.float32)
            ).astype(jnp.bfloat16)
            third[g].start()

        for g in range(groups):
            produce(g)
            first[g].start()
            second[g].start()
            if g > 0:
                relay(g - 1)
        relay(groups - 1)
        for g in range(groups):
            second[g].wait_recv()
            third[g].wait_recv()
            conclude(g, [flank[g], crossed[g]])
        sent = sent + first + second + third
    else:
        landed, r_send, r_recv = scratch
        moves = []
        for g in range(groups):
            produce(g)
            move = [
                head_copy(part.at[g, peer], landed.at[p, g], r_send.at[p, g], r_recv.at[p, g], peer)
                for p, peer in enumerate(head_peers)
            ]
            for copy in move:
                copy.start()
            moves.append(move)
        for g in range(groups):
            for copy in moves[g]:
                copy.wait_recv()
            conclude(g, [landed[p, g] for p in range(n - 1)])
        sent = sent + [copy for move in moves for copy in move]

    for copy in sent:
        copy.wait_send()
    for slot in range(slots):

        @pl.when(gives[slot])
        def _():
            for j in range(2 * per_part):
                halo_copy(slot, j).wait_send()


def on_device(
    n,
    peers,
    tokens,
    in_sign,
    qkv_codes,
    qkv_scale,
    qkv_sign,
    windows,
    oin_sign,
    out_codes,
    out_scale,
    out_sign,
):
    own = tokens[0]
    rows, width = own.shape
    local = qkv_scale.shape[1]
    features = out_codes.shape[1]
    reach = (1,) if peers <= HROWS else (1, HROWS - 1, HROWS, HROWS + 1)
    distances = tuple(d for r in reach if r < peers for d in (r, -r))
    slots = len(distances)
    cols = 256 if local % 256 == 0 else HD
    count = 3 * local // cols
    per_part = count // 3
    inner = qkv_codes.shape[0]
    gcols = 1024 if features % 1024 == 0 else HD
    groups = features // gcols
    share = rows // n
    chunks = 4
    dma = pltpu.SemaphoreType.DMA
    grouped = pltpu.VMEM((groups, share, gcols), jnp.bfloat16)
    if n == 4:
        tail = [dma((chunks,))] * 4 + [dma] * 2 + [grouped] * 4 + [dma((groups,))] * 6
    else:
        tail = [dma((n - 1,))] * 2
        tail += [pltpu.VMEM((n - 1, groups, share, gcols), jnp.bfloat16)]
        tail += [dma((n - 1, groups))] * 2
    vmem = pl.BlockSpec(memory_space=pltpu.VMEM)
    anywhere = pl.BlockSpec(memory_space=pl.ANY)
    smem = pl.BlockSpec(memory_space=pltpu.SMEM)
    result = pl.pallas_call(
        functools.partial(layer_kernel, n, peers, distances, cols, gcols),
        name="layer",
        out_shape=jax.ShapeDtypeStruct((share, features), jnp.bfloat16),
        in_specs=[vmem] * 4 + [smem] + [vmem] * 7 + [anywhere] * 2,
        out_specs=vmem,
        scratch_shapes=[
            pltpu.VMEM((n, rows, width), jnp.bfloat16),
            pltpu.VMEM((count, inner, cols), jnp.int32),
            pltpu.VMEM((count, n, width, cols), jnp.bfloat16),
            pltpu.VMEM((count, rows, cols), jnp.float32),
            pltpu.VMEM((rows, HD), jnp.float32),
            pltpu.VMEM((count, rows, cols), jnp.bfloat16),
            pltpu.VMEM((slots, 2 * per_part, rows, cols), jnp.bfloat16),
            pltpu.VMEM(out_codes.shape, jnp.int32),
            pltpu.VMEM((groups, local, gcols), jnp.bfloat16),
            pltpu.VMEM((local // HD, rows, HD), jnp.float32),
            pltpu.VMEM((local // HD, rows, HD), jnp.float32),
            pltpu.VMEM((rows, local), jnp.bfloat16),
            pltpu.VMEM((rows, HD), jnp.float32),
            pltpu.VMEM((count, 16, cols), jnp.float32),
            pltpu.VMEM((n, 8, width), jnp.float32),
            pltpu.VMEM((groups, n, share, gcols), jnp.bfloat16),
            dma((count,)),
            dma,
            dma((slots, 2 * per_part)),
            dma((slots, 2 * per_part)),
        ]
        + tail,
        compiler_params=pltpu.CompilerParams(
            collective_id=0, has_side_effects=True, vmem_limit_bytes=VLIMIT
        ),
    )(
        own,
        in_sign,
        qkv_scale,
        qkv_sign,
        jnp.transpose(windows, (1, 0, 2)),
        oin_sign,
        out_scale,
        out_sign,
        plane_matrix(),
        plain_matrix(),
        plane_scale(),
        plane_power(),
        jnp.transpose(qkv_codes, (1, 0, 2)),
        out_codes,
    )
    return result[None]


def solution(mesh):
    n = mesh.shape["head"]
    peers = mesh.shape["height"]
    return jax.shard_map(
        functools.partial(on_device, n, peers),
        mesh=mesh,
        in_specs=(
            P(("clip", "height"), None, "head"),
            P(),
            P(None, None, "head"),
            P(None, "head"),
            P(None, "head"),
            P(("clip", "height"), None, None),
            P("head"),
            P("head", None),
            P(),
            P(),
        ),
        out_specs=P(("clip", "height"), "head", None),
        check_vma=False,
    )
```

```python
import functools

import jax
import jax.numpy as jnp
import numpy as np
from jax import lax
from jax.experimental import pallas as pl
from jax.experimental.pallas import tpu as pltpu
from jax.sharding import PartitionSpec as P

HD = 128
HAD = 128
TILE = 64
HROWS = 4
PLANES = 8
GROUP = HAD // PLANES
EPSILON = 1e-06
MESH = pl.DeviceIdType.MESH
VLIMIT = 60 * 1024 * 1024


def sylvester(order_size):
    matrix_now = np.ones((1, 1), np.float32)
    seed_pair = np.array([[1.0, 1.0], [1.0, -1.0]], np.float32)
    while matrix_now.shape[0] < order_size:
        matrix_now = np.kron(matrix_now, seed_pair)
    return matrix_now


ORDER = np.array([8 * i + k for k in range(PLANES) for i in range(GROUP)])
PLANE_POWER = np.array([4.0**k for k in range(PLANES) for _ in range(GROUP)], np.float32)


def plain_matrix():
    return jnp.asarray(sylvester(HAD), jnp.bfloat16)


def plane_matrix():
    return jnp.asarray(sylvester(HAD)[:, ORDER], jnp.bfloat16)


def plane_scale():
    return jnp.asarray((HAD**-0.5 / PLANE_POWER)[None, :], jnp.float32)


def plane_power():
    return jnp.asarray(PLANE_POWER[None, :], jnp.float32)


def signed(sign_bits):
    return (2 * sign_bits - 1).astype(jnp.float32)


def dot(left, right):
    return jnp.dot(left, right, preferred_element_type=jnp.float32)


def rotate_split(block, matrix):
    high = block.astype(jnp.bfloat16)
    low = (block - high.astype(jnp.float32)).astype(jnp.bfloat16)
    return (dot(high, matrix) + dot(low, matrix)) * HAD**-0.5


def unpack_block(words):
    planes = [(words & (3 << (2 * k))).astype(jnp.float32).astype(jnp.bfloat16) for k in range(PLANES)]
    pieces = []
    for block in range(words.shape[0] // GROUP):
        for k in range(PLANES):
            pieces.append(planes[k][block * GROUP : (block + 1) * GROUP])
    return jnp.concatenate(pieces, axis=0)


def row_sums(rows, power):
    total = None
    for block in range(rows.shape[1] // HAD):
        part = rows[:, block * HAD : (block + 1) * HAD].astype(jnp.float32) * power
        total = part if total is None else total + part
    return jnp.sum(total, axis=1, keepdims=True)


def layer_kernel(
    n, peers, distances, cols, gcols,
    x_ref, insigns_ref, qscale_ref, qsign_ref, listed_ref, osign_ref, oscale_ref, outsign_ref,
    plane_mat_ref, mat_ref, pscale_ref, power_ref, codes_ref, ocodes_ref,
    out_ref,
    turned, words, weights, acc, offset, qkv, near, owords, oweights, gathered, totals,
    rotated, ooffset, lines, insigns, part, word_sem, oword_sem, halo_send, halo_recv, *scratch,
):
    me = lax.axis_index("head")
    row = lax.axis_index("height")
    rows, width = x_ref.shape
    count = words.shape[0]
    per_part = count // 3
    per_chunk = cols // HD
    local = per_part * cols
    depth = width // PLANES
    qtiles = rows // TILE
    groups = part.shape[0]
    share = rows // n
    slots = len(distances)

    def fetch(j):
        return pltpu.make_async_copy(
            codes_ref.at[(j // per_part + 1) % 3, :, pl.ds(pl.multiple_of(j % per_part * cols, HD), cols)],
            words.at[j],
            word_sem.at[j],
        )

    for j in range(count):
        fetch(j).start()
    fetch_out = pltpu.make_async_copy(ocodes_ref, owords, oword_sem)
    fetch_out.start()

    barrier = pltpu.get_barrier_semaphore()
    if n == 4:
        partner = me + 1 - 2 * (me % 2)
        across = (me + 2) % 4
        diagonal = (partner + 2) % 4
        head_peers = [partner, across]
        early, late = [me, partner], [across, diagonal]
    else:
        head_peers = [(me + p) % n for p in range(1, n)]
        early, late = [me], head_peers
    gives = [jnp.logical_and(row + d >= 0, row + d < peers) for d in distances]
    takes = [jnp.logical_and(row - d >= 0, row - d < peers) for d in distances]
    for peer in head_peers:
        pl.semaphore_signal(barrier, inc=1, device_id={"head": peer}, device_id_type=MESH)
    greeted = jnp.int32(len(head_peers))
    for slot, distance in enumerate(distances):

        @pl.when(gives[slot])
        def _():
            pl.semaphore_signal(
                barrier, inc=1, device_id={"height": row + distance}, device_id_type=MESH
            )

        greeted = greeted + jnp.where(gives[slot], 1, 0)

    for shard in range(n):
        for block in range(width // HAD):
            lanes = slice(block * HAD, (block + 1) * HAD)
            line = signed(insigns_ref[shard * width + block * HAD : shard * width + (block + 1) * HAD])
            insigns[shard, :, lanes] = jnp.broadcast_to(line[None, :], (8, HAD))
    for block in range(width // HAD):
        lanes = slice(block * HAD, (block + 1) * HAD)
        spun = dot(x_ref[:, lanes] * insigns[me, 0:1, lanes].astype(jnp.bfloat16), plane_mat_ref[...])
        turned[me, :, lanes] = (spun * pscale_ref[...]).astype(jnp.bfloat16)
    for j in range(count):
        source = (j // per_part + 1) % 3
        spots = slice(j % per_part * cols, (j % per_part + 1) * cols)
        scale = qscale_ref[source : source + 1, spots] * (width * n) ** -0.5
        sign = signed(qsign_ref[source : source + 1, spots])
        lines[j, 0:8, :] = jnp.broadcast_to(scale, (8, cols))
        lines[j, 8:16, :] = jnp.broadcast_to(sign, (8, cols))
    pl.semaphore_wait(barrier, greeted)

    def head_copy(src, dst, send, recv, peer):
        return pltpu.make_async_remote_copy(
            src, dst, send, recv, device_id={"head": peer}, device_id_type=MESH
        )

    def unpack(j):
        fetch(j).wait()
        for shard in range(n):
            weights[j, shard] = unpack_block(words[j, shard * depth : (shard + 1) * depth, :])
        total = dot(turned[early[0]], weights[j, early[0]])
        for shard in early[1:]:
            total = total + dot(turned[shard], weights[j, shard])
        acc[j] = total

    if n == 4:
        a_send, a_recv, f_send, f_recv, b_send, b_recv = scratch[:6]
        scratch = scratch[6:]
        chunks = a_send.shape[0]
        step = rows // chunks

        def piece(slot, c):
            return turned.at[slot, pl.ds(c * step, step), :]

        crossing = [
            head_copy(piece(me, c), piece(me, c), a_send.at[c], a_recv.at[c], across)
            for c in range(chunks)
        ]
        relays = [
            head_copy(piece(across, c), piece(across, c), f_send.at[c], f_recv.at[c], partner)
            for c in range(chunks)
        ]
        for copy in crossing:
            copy.start()
        beside = head_copy(turned.at[me], turned.at[me], b_send, b_recv, partner)
        beside.start()
        beside.wait_recv()
        done = 0
        for c in range(chunks):
            upto = count * (c + 1) // chunks

            @pl.loop(done, upto)
            def _(j):
                unpack(j)

            done = upto
            crossing[c].wait_recv()
            relays[c].start()
        for copy in relays:
            copy.wait_recv()
        sent = crossing + relays + [beside]
    else:
        g_send, g_recv = scratch[:2]
        scratch = scratch[2:]
        sent = [
            head_copy(turned.at[me], turned.at[me], g_send.at[p], g_recv.at[p], peer)
            for p, peer in enumerate(head_peers)
        ]
        for copy in sent:
            copy.start()

        @pl.loop(0, count)
        def _(j):
            unpack(j)

        for copy in sent:
            copy.wait_recv()

    total = jnp.zeros((rows, 1), jnp.float32)
    for shard in range(n):
        total = total + row_sums(turned[shard], power_ref[...])
    offset[...] = jnp.broadcast_to(1.5 * total, offset.shape)

    def finish(j):
        result = acc[j]
        for shard in late:
            result = result + dot(turned[shard], weights[j, shard])
        source = (j // per_part + 1) % 3
        for head in range(per_chunk):
            lanes = slice(head * HD, (head + 1) * HD)
            block = (result[:, lanes] - offset[...]) * lines[j, 0:1, lanes]
            block = rotate_split(block, mat_ref[...]) * lines[j, 8:9, lanes]
            mean = jnp.mean(block * block, axis=-1, keepdims=True)
            divisor = jnp.where(source < 2, jnp.sqrt(mean + EPSILON), 1.0)
            qkv[j, :, lanes] = (block / divisor).astype(jnp.bfloat16)

    def halo_copy(slot, j):
        return pltpu.make_async_remote_copy(
            qkv.at[j], near.at[slot, j], halo_send.at[slot, j], halo_recv.at[slot, j],
            device_id={"height": row + distances[slot]}, device_id_type=MESH,
        )

    @pl.loop(0, 2 * per_part)
    def _(j):
        finish(j)
        for slot in range(slots):

            @pl.when(gives[slot])
            def _():
                halo_copy(slot, j).start()

    for slot in range(slots):

        @pl.when(jnp.logical_not(takes[slot]))
        def _():
            near[slot] = jnp.zeros(near.shape[1:], near.dtype)

    @pl.loop(2 * per_part, count)
    def _(j):
        finish(j)

    def mask_of(first_tile):
        ids = lax.broadcasted_iota(jnp.int32, (8, rows), 1) // TILE + first_tile
        stack = []
        for tile in range(qtiles):
            hit = ids == listed_ref[tile, 0, 0]
            for entry in range(1, listed_ref.shape[2]):
                hit = jnp.logical_or(hit, ids == listed_ref[tile, 0, entry])
            stack.extend([jnp.where(hit, 1.0, 0.0)] * (TILE // 8))
        return jnp.concatenate(stack, axis=0)

    def attend(queries, keys, values, mask):
        score = lax.dot_general(
            queries, keys, (((1,), (1,)), ((), ())), preferred_element_type=jnp.float32
        )
        weight = jnp.exp(score * HD**-0.5) * mask
        return dot(weight.astype(jnp.bfloat16), values), jnp.sum(weight, axis=-1, keepdims=True)

    own_mask = mask_of(row * qtiles)
    near_masks = [mask_of((row - d) * qtiles) for d in distances]
    for head in range(local // HD):
        chunk, lanes = head // per_chunk, slice(head % per_chunk * HD, (head % per_chunk + 1) * HD)
        found, sums = attend(
            qkv[2 * per_part + chunk, :, lanes], qkv[chunk, :, lanes],
            qkv[per_part + chunk, :, lanes], own_mask,
        )
        gathered[head] = found
        totals[head] = jnp.broadcast_to(sums, found.shape)

    fetch_out.wait()

    @pl.loop(0, groups)
    def _(g):
        spots = pl.ds(pl.multiple_of(g * gcols, HD), gcols)
        oweights[g] = unpack_block(owords[:, spots])

    for head in range(local // HD):
        chunk, lanes = head // per_chunk, slice(head % per_chunk * HD, (head % per_chunk + 1) * HD)
        if head % per_chunk == 0:
            for slot in range(slots):

                @pl.when(takes[slot])
                def _():
                    halo_copy(slot, chunk).wait_recv()
                    halo_copy(slot, per_part + chunk).wait_recv()

        found, sums = gathered[head], totals[head]
        for slot in range(slots):
            more, more_sums = attend(
                qkv[2 * per_part + chunk, :, lanes], near[slot, chunk, :, lanes],
                near[slot, per_part + chunk, :, lanes], near_masks[slot],
            )
            found, sums = found + more, sums + more_sums
        attended = (found / sums).astype(jnp.bfloat16)
        spots = slice(head * HD, (head + 1) * HD)
        spun = dot(attended * signed(osign_ref[spots])[None, :].astype(jnp.bfloat16), plane_mat_ref[...])
        rotated[:, spots] = (spun * pscale_ref[...]).astype(jnp.bfloat16)
    ooffset[...] = jnp.broadcast_to(1.5 * row_sums(rotated[...], power_ref[...]), ooffset.shape)

    def produce(g):
        result = dot(rotated[...], oweights[g])
        for block in range(gcols // HAD):
            lanes = slice(block * HAD, (block + 1) * HAD)
            spots = slice(g * gcols + block * HAD, g * gcols + (block + 1) * HAD)
            value = (result[:, lanes] - ooffset[...]) * (oscale_ref[spots] * (local * n) ** -0.5)[None, :]
            part[g, :, :, lanes] = value.reshape(n, share, HAD).astype(jnp.bfloat16)

    def conclude(g, terms):
        for block in range(gcols // HAD):
            lanes = slice(block * HAD, (block + 1) * HAD)
            spots = slice(g * gcols + block * HAD, g * gcols + (block + 1) * HAD)
            total = part[g, me, :, lanes].astype(jnp.float32)
            for term in terms:
                total = total + term[:, lanes].astype(jnp.float32)
            spun = rotate_split(total, mat_ref[...]) * signed(outsign_ref[spots])[None, :]
            out_ref[:, spots] = spun.astype(jnp.bfloat16)

    if n == 4:
        staged, flank, summed, crossed, p_send, p_recv, q_send, q_recv, x_send, x_recv = scratch
        first = [
            head_copy(part.at[g, diagonal], staged.at[g], p_send.at[g], p_recv.at[g], partner)
            for g in range(groups)
        ]
        second = [
            head_copy(part.at[g, partner], flank.at[g], q_send.at[g], q_recv.at[g], partner)
            for g in range(groups)
        ]
        third = [
            head_copy(summed.at[g], crossed.at[g], x_send.at[g], x_recv.at[g], across)
            for g in range(groups)
        ]

        def relay(g):
            first[g].wait_recv()
            summed[g] = (
                part[g, across].astype(jnp.float32) + staged[g].astype(jnp.float32)
            ).astype(jnp.bfloat16)
            third[g].start()

        for g in range(groups):
            produce(g)
            first[g].start()
            second[g].start()
            if g > 0:
                relay(g - 1)
        relay(groups - 1)
        for g in range(groups):
            second[g].wait_recv()
            third[g].wait_recv()
            conclude(g, [flank[g], crossed[g]])
        sent = sent + first + second + third
    else:
        landed, r_send, r_recv = scratch
        moves = []
        for g in range(groups):
            produce(g)
            move = [
                head_copy(part.at[g, peer], landed.at[p, g], r_send.at[p, g], r_recv.at[p, g], peer)
                for p, peer in enumerate(head_peers)
            ]
            for copy in move:
                copy.start()
            moves.append(move)
        for g in range(groups):
            for copy in moves[g]:
                copy.wait_recv()
            conclude(g, [landed[p, g] for p in range(n - 1)])
        sent = sent + [copy for move in moves for copy in move]

    for copy in sent:
        copy.wait_send()
    for slot in range(slots):

        @pl.when(gives[slot])
        def _():
            for j in range(2 * per_part):
                halo_copy(slot, j).wait_send()


def on_device(
    n,
    peers,
    tokens,
    in_sign,
    qkv_codes,
    qkv_scale,
    qkv_sign,
    windows,
    oin_sign,
    out_codes,
    out_scale,
    out_sign,
):
    own = tokens[0]
    rows, width = own.shape
    local = qkv_scale.shape[1]
    features = out_codes.shape[1]
    reach = (1,) if peers <= HROWS else (1, HROWS - 1, HROWS, HROWS + 1)
    distances = tuple(d for r in reach if r < peers for d in (r, -r))
    slots = len(distances)
    cols = 256 if local % 256 == 0 else HD
    count = 3 * local // cols
    per_part = count // 3
    inner = qkv_codes.shape[0]
    gcols = 1024 if features % 1024 == 0 else HD
    groups = features // gcols
    share = rows // n
    chunks = 4
    dma = pltpu.SemaphoreType.DMA
    grouped = pltpu.VMEM((groups, share, gcols), jnp.bfloat16)
    if n == 4:
        tail = [dma((chunks,))] * 4 + [dma] * 2 + [grouped] * 4 + [dma((groups,))] * 6
    else:
        tail = [dma((n - 1,))] * 2
        tail += [pltpu.VMEM((n - 1, groups, share, gcols), jnp.bfloat16)]
        tail += [dma((n - 1, groups))] * 2
    vmem = pl.BlockSpec(memory_space=pltpu.VMEM)
    anywhere = pl.BlockSpec(memory_space=pl.ANY)
    smem = pl.BlockSpec(memory_space=pltpu.SMEM)
    result = pl.pallas_call(
        functools.partial(layer_kernel, n, peers, distances, cols, gcols),
        name="layer",
        out_shape=jax.ShapeDtypeStruct((share, features), jnp.bfloat16),
        in_specs=[vmem] * 4 + [smem] + [vmem] * 7 + [anywhere] * 2,
        out_specs=vmem,
        scratch_shapes=[
            pltpu.VMEM((n, rows, width), jnp.bfloat16),
            pltpu.VMEM((count, inner, cols), jnp.int32),
            pltpu.VMEM((count, n, width, cols), jnp.bfloat16),
            pltpu.VMEM((count, rows, cols), jnp.float32),
            pltpu.VMEM((rows, HD), jnp.float32),
            pltpu.VMEM((count, rows, cols), jnp.bfloat16),
            pltpu.VMEM((slots, 2 * per_part, rows, cols), jnp.bfloat16),
            pltpu.VMEM(out_codes.shape, jnp.int32),
            pltpu.VMEM((groups, local, gcols), jnp.bfloat16),
            pltpu.VMEM((local // HD, rows, HD), jnp.float32),
            pltpu.VMEM((local // HD, rows, HD), jnp.float32),
            pltpu.VMEM((rows, local), jnp.bfloat16),
            pltpu.VMEM((rows, HD), jnp.float32),
            pltpu.VMEM((count, 16, cols), jnp.float32),
            pltpu.VMEM((n, 8, width), jnp.float32),
            pltpu.VMEM((groups, n, share, gcols), jnp.bfloat16),
            dma((count,)),
            dma,
            dma((slots, 2 * per_part)),
            dma((slots, 2 * per_part)),
        ]
        + tail,
        compiler_params=pltpu.CompilerParams(
            collective_id=0, has_side_effects=True, vmem_limit_bytes=VLIMIT
        ),
    )(
        own,
        in_sign,
        qkv_scale,
        qkv_sign,
        jnp.transpose(windows, (1, 0, 2)),
        oin_sign,
        out_scale,
        out_sign,
        plane_matrix(),
        plain_matrix(),
        plane_scale(),
        plane_power(),
        jnp.transpose(qkv_codes, (1, 0, 2)),
        out_codes,
    )
    return result[None]


def solution(mesh):
    n = mesh.shape["head"]
    peers = mesh.shape["height"]
    return jax.shard_map(
        functools.partial(on_device, n, peers),
        mesh=mesh,
        in_specs=(
            P(("clip", "height"), None, "head"),
            P(),
            P(None, None, "head"),
            P(None, "head"),
            P(None, "head"),
            P(("clip", "height"), None, None),
            P("head"),
            P("head", None),
            P(),
            P(),
        ),
        out_specs=P(("clip", "height"), "head", None),
        check_vma=False,
    )
```
